512 devices in a mesh: wide: 64 (over z, y_hi, core), narrow: 8 (over x, y_lo).
Axes of the slice: x: 4, y: 4 (y_hi: 2, y_lo: 2; y = y_hi * 2 + y_lo), z: 16, core: 2. Of those that a mesh axis runs over, the one named last changes fastest.
Arguments:
- stiffness: bfloat16 [512, 1024, 1024], P(('wide', 'narrow')), may hold values from -0.125625 to 5, as said below
- load_cases: bfloat16 [512, 1024, 256], P(('wide', 'narrow')), may hold values from -6 to 6
- coarse_inverse: bfloat16 [8192, 8192], P('wide', 'narrow'), may hold values from -0.0011600971 to 0.015625
- face_index: int32 [512, 4, 128], P(('wide', 'narrow')), may hold values from 0 to 1023, as said below
- face_count: int32 [512, 4, 128], P(('wide', 'narrow')), may hold values from 1 to 3, as said below
- aggregate: int32 [512, 1024], P(('wide', 'narrow')), may hold values from 0 to 15
Outputs:
- solution: float32 [512, 1024, 256], P(('wide', 'narrow'))
- coarse: float32 [8192, 256], P(('wide', 'narrow'))
The draws below stay inside these ranges and needn't reach their ends.
Inputs may be any that keep to these rules, and one draw needn't show every extreme that they name: `face_index`: the 512 entries of one cell are distinct. face_count[c, 1, s] + face_count[c2, 0, s] = 4 where c2 is the cell of the next brick column in the same row, and face_count[c, 3, s] + face_count[c3, 2, s] = 4 where c3 is the cell of the next brick row in the same column. `stiffness`: each cell's matrix is symmetric.
All inputs are finite; a program needn't handle non-finite values.
Results may differ from the reference program's by a relative error of at most 0.018.
Values may be sent and summed in bfloat16 or wider, within the bound.
A program may use at most 64 MiB of HBM per device.

```python
import math
import jax
import jax.numpy as jnp
from jax import lax

ORDER = 1024
FACE = 128
AGG = 16
LOADS = 256
CHEB = 4
ITERS = 2
CELL_COLS = 64
CELL_ROWS = 8
CELLS = 512
COARSE = 8192


def draw_stiffness(key, part):

    def one_matrix(cell_key):
        first, second = jax.random.split(cell_key)
        upper_part = jnp.clip(jax.random.normal(first, (ORDER, ORDER), jnp.float32), -4.0, 4.0)
        diag_vals = jax.random.uniform(second, (ORDER,), jnp.float32, 3.2, 4.8)
        upper_part = jnp.triu(upper_part, 1) / math.sqrt(ORDER)
        return (upper_part + upper_part.T + jnp.diag(diag_vals)).astype(jnp.bfloat16)
    return lax.map(one_matrix, jax.random.split(key, CELLS))


def draw_coarse_inverse(key, part):
    first, second, third = jax.random.split(key, 3)
    noise = jnp.clip(jax.random.normal(first, (COARSE, COARSE), jnp.float32), -4.0, 4.0)
    scales = jnp.exp(jax.random.uniform(second, (CELLS,), jnp.float32, 0.0, math.log(10.0)))
    column_scale = jnp.repeat(scales, AGG)
    diag_vals = jax.random.uniform(third, (COARSE,), jnp.float32, 0.0078125, 0.015625)
    offdiag = noise * column_scale[None, :] * (0.0026 / math.sqrt(COARSE))
    row_ids = jnp.arange(COARSE, dtype=jnp.int32)
    cell_ids = row_ids // AGG
    member = row_ids % AGG
    target = (cell_ids % CELL_ROWS * CELL_COLS + cell_ids // CELL_ROWS) * AGG + member
    placed = target[:, None] == row_ids[None, :]
    return jnp.where(placed, diag_vals[:, None], offdiag).astype(jnp.bfloat16)


def draw_face_index(key, part):

    def one_cell(cell_key):
        return jax.random.permutation(cell_key, ORDER)[:4 * FACE].astype(jnp.int32).reshape(4, FACE)
    return jax.vmap(one_cell)(jax.random.split(key, CELLS))


def draw_face_count(key, part):
    first, second, third, fourth = jax.random.split(key, 4)
    rightward = jax.random.randint(first, (CELL_COLS, CELL_ROWS, FACE), 1, 4)
    edge_left = jax.random.randint(second, (1, CELL_ROWS, FACE), 1, 4)
    leftward = jnp.concatenate([edge_left, 4 - rightward[:-1]], axis=0)
    upward = jax.random.randint(third, (CELL_COLS, CELL_ROWS, FACE), 1, 4)
    edge_down = jax.random.randint(fourth, (CELL_COLS, 1, FACE), 1, 4)
    downward = jnp.concatenate([edge_down, 4 - upward[:, :-1]], axis=1)
    stacked = jnp.stack([leftward, rightward, downward, upward], axis=2)
    return stacked.reshape(CELLS, 4, FACE).astype(jnp.int32)


def place_ends(values, key, low, top_value):
    extent = values.shape
    index_at = [jax.random.randint(jax.random.fold_in(key, axis), (), 0, extent[axis]) for axis in range(len(extent))]
    values = values.at[tuple(index_at)].set(low)
    longest = extent.index(max(extent))
    index_at[longest] = (index_at[longest] + 1) % extent[longest]
    return values.at[tuple(index_at)].set(top_value)


def shard_levels(own_key, shape, shards, least, top_value):
    def one(dim, shards_of):
        steps = jax.random.uniform(jax.random.fold_in(jax.random.fold_in(own_key, 6), dim), (shards_of,), jnp.float32, least / len(shards), top_value / len(shards))
        return jnp.repeat(jnp.exp(steps), shape[dim] // shards_of).reshape((-1,) + (1,) * (len(shape) - dim - 1))

    level = one(*shards[0])
    for cut in shards[1:]:
        level = level * one(*cut)
    return level


def scatter_about(stream_key, shape, scale, most, shards=(), held_as=jnp.bfloat16):
    array = jax.random.normal(stream_key, shape, jnp.float32) * scale
    if len(shards) > 0:
        array = shard_levels(stream_key, shape, shards, -0.22, 0.18) * array
    return jnp.clip(array, min=-most, max=most).astype(held_as)


def setup_inputs(seed: int = 0) -> dict:
    seeds = jax.random.split(jax.random.key(seed), 7)
    stiffness = draw_stiffness(jax.random.fold_in(seeds[6], 71), 0)
    load_cases = scatter_about(seeds[1], (CELLS, ORDER, LOADS), 1.0, 6.0, ((0, 512),))
    coarse_inverse = draw_coarse_inverse(jax.random.fold_in(seeds[6], 71), 0)
    face_index = draw_face_index(jax.random.fold_in(seeds[6], 71), 0)
    face_count = draw_face_count(jax.random.fold_in(seeds[6], 71), 0)
    aggregate = place_ends(jax.random.randint(seeds[5], (CELLS, ORDER), 0, AGG), jax.random.fold_in(seeds[5], 1), 0, AGG - 1).astype(jnp.int32)
    return dict(stiffness=stiffness, load_cases=load_cases, coarse_inverse=coarse_inverse, face_index=face_index, face_count=face_count, aggregate=aggregate)


lower_bound = 0.8
upper_bound = 7.5


def chebyshev(matrix, residual):
    center = 0.5 * (upper_bound + lower_bound)
    spread = 0.5 * (upper_bound - lower_bound)
    sigma_ratio = center / spread
    rho_old = 1.0 / sigma_ratio
    direction = residual / center
    result = direction
    remain = residual
    for sweep_index in range(CHEB - 1):
        remain = remain - jnp.dot(matrix, direction.astype(jnp.bfloat16), preferred_element_type=jnp.float32)
        rho_new = 1.0 / (2.0 * sigma_ratio - rho_old)
        direction = (rho_new * rho_old) * direction + (2.0 * rho_new / spread) * remain
        result = result + direction
        rho_old = rho_new
    return result


def chebyshev_cell(operands):
    return chebyshev(operands[0], operands[1])


def apply_matrix(operands):
    return jnp.dot(operands[0], operands[1], preferred_element_type=jnp.float32)


def place_rows(matrix, row_index, values):
    return matrix.at[row_index].set(values)


def average_faces(correction, flat_index, weights):
    traces = jnp.take_along_axis(correction, flat_index[:, :, None], axis=1)
    rounded = lax.optimization_barrier(traces.astype(jnp.bfloat16)).astype(jnp.float32)
    rounded = rounded.reshape(CELL_COLS, CELL_ROWS, 4, FACE, -1)
    zero_column = jnp.zeros_like(rounded[:1, :, 0])
    from_left = jnp.concatenate([zero_column, rounded[:-1, :, 1]], axis=0)
    from_right = jnp.concatenate([rounded[1:, :, 0], zero_column], axis=0)
    zero_row = jnp.zeros_like(rounded[:, :1, 2])
    from_below = jnp.concatenate([zero_row, rounded[:, :-1, 3]], axis=1)
    from_above = jnp.concatenate([rounded[:, 1:, 2], zero_row], axis=1)
    neighbour = jnp.stack([from_left, from_right, from_below, from_above], axis=2)
    neighbour = neighbour.reshape(CELLS, 4 * FACE, -1)
    blended = traces + weights[:, :, None] * (neighbour - traces)
    return jax.vmap(place_rows)(correction, flat_index, blended)


def reference(stiffness, load_cases, coarse_inverse, face_index, face_count, aggregate):
    loads_float = load_cases.astype(jnp.float32)
    solution = jnp.zeros(loads_float.shape, jnp.float32)
    members = jnp.arange(AGG, dtype=jnp.int32)
    onehot = (aggregate[:, None, :] == members[None, :, None]).astype(jnp.float32)
    column = jnp.arange(CELL_COLS, dtype=jnp.int32)[:, None] + jnp.zeros((1, CELL_ROWS), jnp.int32)
    brick_row = jnp.arange(CELL_ROWS, dtype=jnp.int32)[None, :] + jnp.zeros((CELL_COLS, 1), jnp.int32)
    present = jnp.stack([column > 0, column < CELL_COLS - 1, brick_row > 0, brick_row < CELL_ROWS - 1], axis=-1)
    present = present.astype(jnp.float32).reshape(CELLS, 4)
    weights = ((4 - face_count).astype(jnp.float32) / 4.0 * present[:, :, None]).reshape(CELLS, 4 * FACE)
    flat_index = face_index.reshape(CELLS, 4 * FACE)
    coarse = jnp.zeros((COARSE, loads_float.shape[2]), jnp.float32)
    for outer_index in range(ITERS):
        if outer_index == 0:
            residual = loads_float
        else:
            residual = loads_float - lax.map(apply_matrix, (stiffness, solution.astype(jnp.bfloat16)))
        coarse_res = jnp.einsum("cko,col->ckl", onehot, residual, precision=lax.Precision.HIGHEST)
        coarse_res = coarse_res.astype(jnp.bfloat16)
        ordered = coarse_res.reshape(CELL_COLS, CELL_ROWS, AGG, -1).transpose(1, 0, 2, 3).reshape(COARSE, -1)
        coarse = jnp.dot(coarse_inverse, ordered, preferred_element_type=jnp.float32)
        correction = lax.map(chebyshev_cell, (stiffness, residual))
        averaged = average_faces(correction, flat_index, weights)
        prolonged = jnp.einsum("cko,ckl->col", onehot, coarse.reshape(CELLS, AGG, -1), precision=lax.Precision.HIGHEST)
        solution = solution + averaged + prolonged
    return solution, coarse
```

```python
import jax
import jax.numpy as jnp
from jax import lax
from jax.experimental import pallas as pl
from jax.experimental.pallas import tpu as pltpu
from jax.sharding import PartitionSpec as P

ORDER = 1024
FACE = 128
AGG = 16
LOADS = 256
CHEB = 4
DEPTH = 16
CLASSES = 4
ROWS = 8
GROUP = CLASSES * ROWS
CHUNK = 256

lower_bound = 0.8
upper_bound = 7.5
center = 0.5 * (upper_bound + lower_bound)
spread = 0.5 * (upper_bound - lower_bound)

f32 = jnp.float32
bf16 = jnp.bfloat16


def steps():
    sigma_ratio = center / spread
    rho_old = 1.0 / sigma_ratio
    factors = []
    for _ in range(CHEB - 1):
        rho_new = 1.0 / (2.0 * sigma_ratio - rho_old)
        factors.append((rho_new * rho_old, 2.0 * rho_new / spread))
        rho_old = rho_new
    return factors


FACTORS = steps()


def offsets():
    every = [(a, b, c) for a in range(4) for b in range(4) for c in range(2)]
    every = [o for o in every if o != (0, 0, 0)]
    return sorted(every, key=lambda o: -(min(o[0], 4 - o[0]) + min(o[1], 4 - o[1])))


OFFSETS = offsets()


def dot(a, b):
    return jnp.dot(a, b, preferred_element_type=f32)


def over_rows(body, size=CHUNK, total=ORDER):
    @pl.loop(0, total // size)
    def _(i):
        body(pl.ds(pl.multiple_of(i * size, size), size))


def split(value):
    high = value.astype(bf16)
    return high, (value - high.astype(f32)).astype(bf16)


def transposed_row(row):
    return jnp.transpose(jnp.broadcast_to(row.astype(f32), (128, 128)))


def fill_prolongation(agg_ref, into):
    lane = lax.broadcasted_iota(jnp.int32, (128, 128), 1)
    member = jnp.where(lane < 2 * AGG, lane % AGG, -1).astype(f32)
    for i in range(ORDER // 128):
        column = transposed_row(agg_ref[:, i * 128 : (i + 1) * 128])
        into[i * 128 : (i + 1) * 128, :] = jnp.where(column == member, 1.0, 0.0).astype(bf16)


def kernel(
    stiffness, loads, inverse, face_index, face_count, aggregate,
    y_ref, coarse_ref,
    K, B, A, q, d, zs, x1, da, db, G, Gw, D, Pm, Pt, PK, S,
    aperm, A2, v1, v2, ys1, ys2, r1, r2, t1, t2, n1, n2, C, pb,
    lsem, asem, arecv, vsend, vrecv, ysend, yrecv, tsend, trecv, osem,
):
    w = lax.axis_index("wide")
    n = lax.axis_index("narrow")
    z = w // 4
    cls = w % 4
    y = ((w // 2) % 2) * 2 + n % 2
    x = n // 2
    core = w % 2

    def along(k):
        return (((z + DEPTH + k) % DEPTH) * 4 + cls, n)

    def depth_rows(k):
        return pl.ds(pl.multiple_of(((z + DEPTH + k) % DEPTH) * AGG, AGG), AGG)

    def member(o):
        yy = (y + o[1]) % 4
        other = (yy // 2) * 2 + (core + o[2]) % 2
        nn = ((x + o[0]) % 4) * 2 + yy % 2
        return (z * 4 + other, nn), other * ROWS + nn

    def group_rows(index):
        return pl.ds(pl.multiple_of(index * AGG, AGG), AGG)

    own = cls * ROWS + n
    sides = [((w + 63) % 64, n), ((w + 1) % 64, n), (w, (n + 7) % 8), (w, (n + 1) % 8)]

    barrier = pltpu.get_barrier_semaphore()
    near = [along(s * k) for k in (4, 3, 2, 1) for s in (1, -1)]
    greeted = near + [member(o)[0] for o in OFFSETS] + sides[:2]
    for peer in greeted:
        pl.semaphore_signal(barrier, inc=1, device_id=peer, device_id_type=pl.DeviceIdType.MESH)

    load_b = pltpu.make_async_copy(loads, B, lsem.at[0])
    load_a = pltpu.make_async_copy(inverse, A, lsem.at[1])
    load_k = pltpu.make_async_copy(stiffness, K, lsem.at[2])
    load_b.start()
    load_a.start()
    load_k.start()

    def send(src, dst, ssem, rsem, peer):
        pltpu.make_async_remote_copy(
            src_ref=src, dst_ref=dst, send_sem=ssem, recv_sem=rsem,
            device_id=peer, device_id_type=pl.DeviceIdType.MESH,
        ).start()

    def wait(ref, sem):
        pltpu.make_async_copy(ref, ref, sem).wait()

    sub16 = lax.broadcasted_iota(jnp.int32, (AGG, ORDER), 0)
    Pm[...] = jnp.where(sub16 == aggregate[...], 1.0, 0.0).astype(bf16)
    load_b.wait()
    first = dot(Pm[...], B[...])
    pb[...] = first
    v1[depth_rows(0), :] = first.astype(bf16)

    load_a.wait()
    for j in range(CLASSES):
        place = lax.broadcasted_iota(jnp.int32, (CHUNK, CHUNK), 1)
        place = (place // AGG) * (CLASSES * AGG) + j * AGG + place % AGG
        row = lax.broadcasted_iota(jnp.int32, (CHUNK, CHUNK), 0)
        total = jnp.zeros((128, CHUNK), f32)
        for t in range(4):
            pick = jnp.where(row + t * CHUNK == place, 1.0, 0.0).astype(bf16)
            total = total + dot(A[:, t * CHUNK : (t + 1) * CHUNK], pick)
        aperm[j] = total.astype(bf16)
    A2[cls] = aperm[cls]

    pl.semaphore_wait(barrier, len(greeted))

    for i, k in enumerate((4, -4, 3, -3, 2, -2, 1, -1)):
        sem = vrecv.at[0] if k == 4 else vrecv.at[1] if k == -4 else vrecv.at[2]
        send(v1.at[depth_rows(0)], v1.at[depth_rows(0)], vsend.at[0], sem, along(k))
    for k in (1, 2, 3):
        other = (cls + k) % 4
        send(aperm.at[other], A2.at[cls], asem, arecv, (z * 4 + other, n))

    lane = lax.broadcasted_iota(jnp.int32, (128, 128), 1).astype(f32)
    sub = lax.broadcasted_iota(jnp.int32, (128, 128), 0).astype(f32)
    there = [w > 0, w < 63, n > 0, n < 7]
    for f in range(4):
        row = face_index[f : f + 1, :].astype(f32)
        column = transposed_row(row)
        weight = (4 - face_count[f : f + 1, :]).astype(f32) * 0.25
        weight = weight * jnp.where(there[f], 1.0, 0.0)
        for i in range(8):
            hit = jnp.where(column == lane + 128.0 * i, 1.0, 0.0)
            G[f * 128 : (f + 1) * 128, i * 128 : (i + 1) * 128] = hit.astype(bf16)
            hit = jnp.where(row == sub + 128.0 * i, weight, 0.0)
            Gw[i * 128 : (i + 1) * 128, f * 128 : (f + 1) * 128] = hit.astype(bf16)

    def chebyshev(after_second):
        def start(rows):
            da[rows, :] = (q[rows, :] * (1.0 / center)).astype(bf16)

        over_rows(start)
        for s, (keep, gain) in enumerate(FACTORS):
            src, dst = (da, db) if s % 2 == 0 else (db, da)

            def step(rows, s=s, keep=keep, gain=gain, src=src, dst=dst):
                before = q[rows, :]
                left = before - dot(K[rows, :], src[...])
                old = before * (1.0 / center) if s == 0 else d[rows, :]
                result = old if s == 0 else zs[rows, :]
                new = keep * old + gain * left
                if s < CHEB - 2:
                    q[rows, :] = left
                    d[rows, :] = new
                zs[rows, :] = result + new
                dst[rows, :] = (new if s < CHEB - 2 else result + new).astype(bf16)

            over_rows(step)
            if s == 1:
                after_second()
        return db

    def trade(corr, t, nb, tsem, rsem):
        t[...] = dot(G[...], corr[...]).astype(bf16)
        for f, target in ((0, 1), (1, 0), (2, 3), (3, 2)):
            send(
                t.at[pl.ds(f * FACE, FACE)], nb.at[pl.ds(target * FACE, FACE)], tsem, rsem,
                sides[f],
            )

    def relay():
        wait(v1.at[depth_rows(-4)], vrecv.at[0])
        for k in (4, 3, 2, 1):
            send(v1.at[depth_rows(-4)], v1.at[depth_rows(-4)], vsend.at[0], vrecv.at[2], along(k))
        wait(v1.at[depth_rows(4)], vrecv.at[1])
        for k in (-3, -2, -1):
            send(v1.at[depth_rows(4)], v1.at[depth_rows(4)], vsend.at[0], vrecv.at[2], along(k))

    def scatter_partials(v, ys, r, ssem, rsem):
        for half in range(2):
            rows = pl.ds(half * CHUNK, CHUNK)
            value = dot(A2[2 * half : 2 * half + 2].reshape(CHUNK, CHUNK), v[...])
            ys[rows, :] = value.astype(bf16)
        for o in OFFSETS:
            peer, index = member(o)
            send(ys.at[group_rows(index)], r.at[group_rows(own)], ssem, rsem, peer)
        r[group_rows(own), :] = ys[group_rows(own), :]

    def gathered_sum(r):
        total = r[0:AGG, :].astype(f32)
        for i in range(1, GROUP):
            total = total + r[i * AGG : (i + 1) * AGG, :].astype(f32)
        return total

    def to_f32(rows):
        q[rows, :] = B[rows, :].astype(f32)

    over_rows(to_f32)
    load_k.wait()
    corr = chebyshev(relay)
    trade(corr, t1, n1, tsend.at[0], trecv.at[0])

    fill_prolongation(aggregate, Pt)
    high, low = split(dot(Pm[...], K[...]))
    PK[0:AGG, :] = high
    PK[AGG : 2 * AGG, :] = low
    both = dot(PK[...], Pt[...])
    high, low = split(both[0:AGG] + both[AGG : 2 * AGG])
    S[0:AGG, :] = high
    S[AGG : 2 * AGG, :] = low
    C[2 * AGG :, :] = jnp.zeros((128 - 2 * AGG, LOADS), bf16)

    wait(v1.at[pl.ds(0, 13 * AGG)], vrecv.at[2])
    wait(A2.at[pl.ds(0, 3)], arecv)
    scatter_partials(v1, ys1, r1, ysend.at[0], yrecv.at[0])

    def keep_share(rows):
        D[rows, :] = 1.0 - dot(Gw[rows, :], jnp.ones((4 * FACE, LOADS), bf16))

    over_rows(keep_share)
    wait(n1, trecv.at[0])

    def average(rows):
        value = D[rows, :] * zs[rows, :] + dot(Gw[rows, :], n1[...])
        x1[rows, :] = value
        da[rows, :] = value.astype(bf16)

    over_rows(average)
    both = dot(PK[...], da[...])
    pb[...] = pb[...] - both[0:AGG] - both[AGG : 2 * AGG]

    wait(r1.at[pl.ds(0, (GROUP - 1) * AGG)], yrecv.at[0])
    high, low = split(gathered_sum(r1))
    C[0:AGG, :] = high
    C[AGG : 2 * AGG, :] = low
    both = dot(S[...], C[...])
    v2[depth_rows(0), :] = (pb[...] - both[0:AGG] - both[AGG : 2 * AGG]).astype(bf16)
    for k in (8, 7, -7, 6, -6, 5, -5, 4, -4, 3, -3, 2, -2, 1, -1):
        send(v2.at[depth_rows(0)], v2.at[depth_rows(0)], vsend.at[1], vrecv.at[3], along(k))

    def prolong(rows):
        value = x1[rows, :] + dot(Pt[rows, :], C[...])
        x1[rows, :] = value
        db[rows, :] = value.astype(bf16)

    over_rows(prolong)

    def residual(rows):
        q[rows, :] = B[rows, :].astype(f32) - dot(K[rows, :], db[...])

    over_rows(residual)
    corr = chebyshev(lambda: None)
    trade(corr, t2, n2, tsend.at[1], trecv.at[1])
    wait(v2.at[pl.ds(0, 15 * AGG)], vrecv.at[3])
    scatter_partials(v2, ys2, r2, ysend.at[1], yrecv.at[1])
    wait(n2, trecv.at[1])

    def finish(rows):
        value = D[rows, :] * zs[rows, :] + dot(Gw[rows, :], n2[...])
        x1[rows, :] = x1[rows, :] + value

    over_rows(finish)
    out = pltpu.make_async_copy(x1, y_ref, osem)
    out.start()
    wait(r2.at[pl.ds(0, (GROUP - 1) * AGG)], yrecv.at[1])
    coarse_ref[...] = gathered_sum(r2)
    out.wait()

    wait(v1.at[pl.ds(0, 15 * AGG)], vsend.at[0])
    wait(aperm.at[pl.ds(0, 3)], asem)
    wait(t1, tsend.at[0])
    wait(ys1.at[pl.ds(0, (GROUP - 1) * AGG)], ysend.at[0])
    wait(v2.at[pl.ds(0, 15 * AGG)], vsend.at[1])
    wait(t2, tsend.at[1])
    wait(ys2.at[pl.ds(0, (GROUP - 1) * AGG)], ysend.at[1])


def closing(y_ref, coarse_ref, aggregate, out_ref, out_coarse, Pt, C):
    i = pl.program_id(0)

    @pl.when(i == 0)
    def _():
        fill_prolongation(aggregate, Pt)
        high, low = split(coarse_ref[...])
        C[0:AGG, :] = high
        C[AGG : 2 * AGG, :] = low
        C[2 * AGG :, :] = jnp.zeros((128 - 2 * AGG, LOADS), bf16)
        out_coarse[...] = coarse_ref[...]

    rows = pl.ds(pl.multiple_of(i * CHUNK, CHUNK), CHUNK)
    out_ref[...] = y_ref[...] + dot(Pt[rows, :], C[...])


def local(stiffness, load_cases, coarse_inverse, face_index, face_count, aggregate):
    vmem = pl.BlockSpec(memory_space=pltpu.VMEM)
    anywhere = pl.BlockSpec(memory_space=pl.ANY)
    wide_f32 = pltpu.VMEM((ORDER, LOADS), f32)
    wide_bf16 = pltpu.VMEM((ORDER, LOADS), bf16)
    square = pltpu.VMEM((CHUNK, LOADS), bf16)
    half = pltpu.VMEM((GROUP * AGG, LOADS), bf16)
    dma = pltpu.SemaphoreType.DMA
    y, coarse = pl.pallas_call(
        kernel,
        out_shape=(
            jax.ShapeDtypeStruct((ORDER, LOADS), f32),
            jax.ShapeDtypeStruct((AGG, LOADS), f32),
        ),
        in_specs=[anywhere, anywhere, anywhere, vmem, vmem, vmem],
        out_specs=(anywhere, vmem),
        scratch_shapes=[
            pltpu.VMEM((ORDER, ORDER), bf16),
            wide_bf16,
            pltpu.VMEM((128, ORDER), bf16),
            wide_f32, wide_f32, wide_f32, wide_f32,
            wide_bf16, wide_bf16,
            pltpu.VMEM((4 * FACE, ORDER), bf16),
            pltpu.VMEM((ORDER, 4 * FACE), bf16),
            wide_f32,
            pltpu.VMEM((AGG, ORDER), bf16),
            pltpu.VMEM((ORDER, 128), bf16),
            pltpu.VMEM((2 * AGG, ORDER), bf16),
            pltpu.VMEM((2 * AGG, 128), bf16),
            pltpu.VMEM((CLASSES, 128, CHUNK), bf16),
            pltpu.VMEM((CLASSES, 128, CHUNK), bf16),
            square, square,
            half, half, half, half, half, half, half, half,
            pltpu.VMEM((128, LOADS), bf16),
            pltpu.VMEM((AGG, LOADS), f32),
            dma((3,)), dma, dma, dma((2,)), dma((4,)),
            dma((2,)), dma((2,)), dma((2,)), dma((2,)), dma,
        ],
        compiler_params=pltpu.CompilerParams(
            collective_id=0, has_side_effects=True, vmem_limit_bytes=60 * 2**20
        ),
        name="schwarz",
    )(stiffness[0], load_cases[0], coarse_inverse, face_index[0], face_count[0], aggregate)

    whole = pl.BlockSpec((AGG, LOADS), lambda i: (0, 0))
    block = pl.BlockSpec((CHUNK, LOADS), lambda i: (i, 0))
    result, coarse = pl.pallas_call(
        closing,
        grid=(ORDER // CHUNK,),
        out_shape=(
            jax.ShapeDtypeStruct((ORDER, LOADS), f32),
            jax.ShapeDtypeStruct((AGG, LOADS), f32),
        ),
        in_specs=[block, whole, pl.BlockSpec((1, ORDER), lambda i: (0, 0))],
        out_specs=(block, whole),
        scratch_shapes=[pltpu.VMEM((ORDER, 128), bf16), pltpu.VMEM((128, LOADS), bf16)],
        name="closing",
    )(y, coarse, aggregate)
    return (result[None], coarse)


def solution(mesh):
    both = ("wide", "narrow")
    placed = (
        P(both, None, None),
        P(both, None, None),
        P("wide", "narrow"),
        P(both, None, None),
        P(both, None, None),
        P(both, None),
    )
    return jax.shard_map(
        local,
        mesh=mesh,
        in_specs=placed,
        out_specs=(P(both, None, None), P(both, None)),
        check_vma=False,
    )
```

```python
import jax
import jax.numpy as jnp
from jax import lax
from jax.experimental import pallas as pl
from jax.experimental.pallas import tpu as pltpu
from jax.sharding import PartitionSpec as P

ORDER = 1024
FACE = 128
AGG = 16
LOADS = 256
CHEB = 4
DEPTH = 16
CLASSES = 4
ROWS = 8
GROUP = 2 * ROWS
CHUNK = 256

lower_bound = 0.8
upper_bound = 7.5
center = 0.5 * (upper_bound + lower_bound)
spread = 0.5 * (upper_bound - lower_bound)

f32 = jnp.float32
bf16 = jnp.bfloat16


def steps():
    sigma_ratio = center / spread
    rho_old = 1.0 / sigma_ratio
    factors = []
    for _ in range(CHEB - 1):
        rho_new = 1.0 / (2.0 * sigma_ratio - rho_old)
        factors.append((rho_new * rho_old, 2.0 * rho_new / spread))
        rho_old = rho_new
    return factors


FACTORS = steps()


def offsets():
    every = [(a, b) for a in range(4) for b in range(4) if (a, b) != (0, 0)]
    return sorted(every, key=lambda o: -(min(o[0], 4 - o[0]) + min(o[1], 4 - o[1])))


OFFSETS = offsets()


def dot(a, b):
    return jnp.dot(a, b, preferred_element_type=f32)


def over_rows(body, size=CHUNK, total=ORDER):
    for i in range(total // size):
        body(slice(i * size, (i + 1) * size))


def split(value):
    high = value.astype(bf16)
    return high, (value - high.astype(f32)).astype(bf16)


def transposed_row(row):
    return jnp.transpose(jnp.broadcast_to(row.astype(f32), (128, 128)))


def fill_prolongation(agg_ref, into):
    lane = lax.broadcasted_iota(jnp.int32, (128, 128), 1)
    member = jnp.where(lane < 2 * AGG, lane % AGG, -1).astype(f32)
    for i in range(ORDER // 128):
        column = transposed_row(agg_ref[:, i * 128 : (i + 1) * 128])
        into[i * 128 : (i + 1) * 128, :] = jnp.where(column == member, 1.0, 0.0).astype(bf16)


def kernel(
    stiffness, loads, inverse, indices, counts, groups,
    y_ref, pt_ref, c_ref, coarse_ref,
    K, B, A, q, d, zs, x1, da, db, G, Gw, D, Pm, Pt, PK, S,
    aggregate, face_index, face_count, aperm, A2, v1, v2, ys1, ys2, r1, r2, t1, t2, n1, n2, C, pb,
    lsem, asem, arecv, vsend, vrecv, csend, crecv, ysend, yrecv, tsend, trecv,
):
    load_b = pltpu.make_async_copy(loads, B, lsem.at[0])
    load_k = pltpu.make_async_copy(stiffness, K, lsem.at[2])
    load_a = pltpu.make_async_copy(inverse, A, lsem.at[1])
    load_g = pltpu.make_async_copy(groups, aggregate, lsem.at[3])
    load_i = pltpu.make_async_copy(indices, face_index, lsem.at[4])
    load_c = pltpu.make_async_copy(counts, face_count, lsem.at[5])
    load_g.start()
    load_b.start()

    w = lax.axis_index("wide")
    n = lax.axis_index("narrow")
    z = w // 4
    y = ((w // 2) % 2) * 2 + n % 2
    x = n // 2
    high = (w // 2) % 2
    core = w % 2

    def along(k):
        return (((z + DEPTH + k) % DEPTH) * 4 + high * 2 + core, n)

    def slot(k):
        return pl.ds((k % DEPTH) * AGG, AGG)

    def member(o):
        yy = (y + o[1]) % 4
        nn = ((x + o[0]) % 4) * 2 + yy % 2
        return (z * 4 + (yy // 2) * 2 + core, nn), (yy // 2) * ROWS + nn

    def group_rows(index):
        return pl.ds(pl.multiple_of(index * AGG, AGG), AGG)

    own = high * ROWS + n
    other_core = (z * 4 + high * 2 + 1 - core, n)
    across = (z * 4 + (1 - high) * 2 + core, n)
    sides = [((w + 63) % 64, n), ((w + 1) % 64, n), (w, (n + 7) % 8), (w, (n + 1) % 8)]

    barrier = pltpu.get_barrier_semaphore()
    greeted = [along(s * k) for k in (4, 3, 2, 1) for s in (1, -1)]
    greeted = greeted + [member(o)[0] for o in OFFSETS] + sides[:2] + [other_core]
    for peer in greeted:
        pl.semaphore_signal(barrier, inc=1, device_id=peer, device_id_type=pl.DeviceIdType.MESH)
    load_k.start()
    load_a.start()
    load_i.start()
    load_c.start()

    def send(src, dst, ssem, rsem, peer):
        pltpu.make_async_remote_copy(
            src_ref=src, dst_ref=dst, send_sem=ssem, recv_sem=rsem,
            device_id=peer, device_id_type=pl.DeviceIdType.MESH,
        ).start()

    def wait(ref, sem):
        pltpu.make_async_copy(ref, ref, sem).wait()

    load_g.wait()
    sub16 = lax.broadcasted_iota(jnp.int32, (AGG, ORDER), 0)
    Pm[...] = jnp.where(sub16 == aggregate[...], 1.0, 0.0).astype(bf16)
    load_b.wait()
    first = dot(Pm[...], B[...])
    v1[core, slot(0), :] = first.astype(bf16)
    pb[...] = first

    pl.semaphore_wait(barrier, len(greeted))

    for k in (4, -4, 3, -3, 2, -2, 1, -1):
        sem = vrecv.at[0] if k == 4 else vrecv.at[1] if k == -4 else vrecv.at[2]
        send(v1.at[core, slot(0)], v1.at[core, slot(-k)], vsend.at[0], sem, along(k))

    load_a.wait()
    for j in range(CLASSES):
        place = lax.broadcasted_iota(jnp.int32, (CHUNK, CHUNK), 1)
        place = ((place // AGG + z) % DEPTH) * (CLASSES * AGG) + j * AGG + place % AGG
        row = lax.broadcasted_iota(jnp.int32, (CHUNK, CHUNK), 0)
        total = jnp.zeros((128, CHUNK), f32)
        for t in range(4):
            pick = jnp.where(row + t * CHUNK == place, 1.0, 0.0).astype(bf16)
            total = total + dot(A[:, t * CHUNK : (t + 1) * CHUNK], pick)
        aperm[j // 2, j % 2] = total.astype(bf16)
    send(aperm.at[1 - high], A2.at[high], asem, arecv, across)
    A2[high] = aperm[high]

    def chebyshev(after_second):
        def begin(rows):
            da[rows, :] = (q[rows, :] * (1.0 / center)).astype(bf16)

        over_rows(begin)
        for s, (keep, gain) in enumerate(FACTORS):
            src, dst = (da, db) if s % 2 == 0 else (db, da)

            def step(rows, s=s, keep=keep, gain=gain, src=src, dst=dst):
                before = q[rows, :]
                left = before - dot(K[rows, :], src[...])
                old = before * (1.0 / center) if s == 0 else d[rows, :]
                result = old if s == 0 else zs[rows, :]
                new = keep * old + gain * left
                if s < CHEB - 2:
                    q[rows, :] = left
                    d[rows, :] = new
                zs[rows, :] = result + new
                dst[rows, :] = (new if s < CHEB - 2 else result + new).astype(bf16)

            over_rows(step)
            if s == 1:
                after_second()
        return db

    def trade(corr, t, nb, tsem, rsem):
        t[...] = dot(G[...], corr[...]).astype(bf16)
        for f, target in ((0, 1), (1, 0), (2, 3), (3, 2)):
            send(
                t.at[pl.ds(f * FACE, FACE)], nb.at[pl.ds(target * FACE, FACE)], tsem, rsem,
                sides[f],
            )

    def relay():
        wait(v1.at[core, slot(-4)], vrecv.at[0])
        for k in (4, 3, 2, 1):
            send(v1.at[core, slot(-4)], v1.at[core, slot(-4 - k)], vsend.at[0], vrecv.at[3], along(k))
        wait(v1.at[core, slot(4)], vrecv.at[1])
        for k in (3, 2, 1):
            send(v1.at[core, slot(4)], v1.at[core, slot(4 + k)], vsend.at[0], vrecv.at[3], along(-k))

    def share(v, first_slot, count, ssem, rsem):
        rows = pl.ds(first_slot * AGG, count * AGG)
        send(v.at[core, rows], v.at[core, rows], ssem, rsem, other_core)

    def coarse_product(v, ys, r, near, nears, far, ssem, rsem, i):
        wait(v.at[core, pl.ds(0, nears * AGG)], vrecv.at[near])
        share(v, 0, 5, csend.at[i], crecv.at[i])
        share(v, 12, 4, csend.at[i], crecv.at[i])
        wait(v.at[core, pl.ds(0, 7 * AGG)], vrecv.at[far])
        share(v, 5, 7, csend.at[i], crecv.at[i])
        if i == 0:
            wait(A2.at[0], arecv)
        mine = dot(A2[:, core].reshape(CHUNK, CHUNK), v[core])
        wait(v.at[core], crecv.at[i])
        value = mine + dot(A2[:, 1 - core].reshape(CHUNK, CHUNK), v[1 - core])
        ys[...] = value.astype(bf16)
        for o in OFFSETS:
            peer, index = member(o)
            send(ys.at[group_rows(index)], r.at[group_rows(own)], ssem, rsem, peer)
        r[group_rows(own), :] = ys[group_rows(own), :]

    def gathered_sum(r):
        total = r[0:AGG, :].astype(f32)
        for i in range(1, GROUP):
            total = total + r[i * AGG : (i + 1) * AGG, :].astype(f32)
        return total

    def to_f32(rows):
        q[rows, :] = B[rows, :].astype(f32)

    over_rows(to_f32)
    load_k.wait()
    corr = chebyshev(relay)

    load_i.wait()
    load_c.wait()
    lane = lax.broadcasted_iota(jnp.int32, (128, 128), 1).astype(f32)
    sub = lax.broadcasted_iota(jnp.int32, (128, 128), 0).astype(f32)
    there = [w > 0, w < 63, n > 0, n < 7]
    for f in range(4):
        row = face_index[f : f + 1, :].astype(f32)
        column = transposed_row(row)
        weight = (4 - face_count[f : f + 1, :]).astype(f32) * 0.25
        weight = weight * jnp.where(there[f], 1.0, 0.0)
        for i in range(8):
            hit = jnp.where(column == lane + 128.0 * i, 1.0, 0.0)
            G[f * 128 : (f + 1) * 128, i * 128 : (i + 1) * 128] = hit.astype(bf16)
            hit = jnp.where(row == sub + 128.0 * i, weight, 0.0)
            Gw[i * 128 : (i + 1) * 128, f * 128 : (f + 1) * 128] = hit.astype(bf16)
    trade(corr, t1, n1, tsend.at[0], trecv.at[0])

    fill_prolongation(aggregate, Pt)
    top, low = split(dot(Pm[...], K[...]))
    PK[0:AGG, :] = top
    PK[AGG : 2 * AGG, :] = low
    both = dot(PK[...], Pt[...])
    top, low = split(both[0:AGG] + both[AGG : 2 * AGG])
    S[0:AGG, :] = top
    S[AGG : 2 * AGG, :] = low
    C[2 * AGG :, :] = jnp.zeros((128 - 2 * AGG, LOADS), bf16)
    pt_ref[...] = Pt[...]

    coarse_product(v1, ys1, r1, 2, 6, 3, ysend.at[0], yrecv.at[0], 0)

    def keep_share(rows):
        D[rows, :] = 1.0 - dot(Gw[rows, :], jnp.ones((4 * FACE, LOADS), bf16))

    over_rows(keep_share)
    wait(n1, trecv.at[0])

    def average(rows):
        value = D[rows, :] * zs[rows, :] + dot(Gw[rows, :], n1[...])
        x1[rows, :] = value
        da[rows, :] = value.astype(bf16)

    over_rows(average)
    both = dot(PK[...], da[...])
    pb[...] = pb[...] - both[0:AGG] - both[AGG : 2 * AGG]

    wait(r1.at[pl.ds(0, (GROUP - 1) * AGG)], yrecv.at[0])
    top, low = split(gathered_sum(r1))
    C[0:AGG, :] = top
    C[AGG : 2 * AGG, :] = low
    both = dot(S[...], C[...])
    v2[core, slot(0), :] = (pb[...] - both[0:AGG] - both[AGG : 2 * AGG]).astype(bf16)
    for k in (8, 7, -7, 6, -6, 5, -5, 4, -4, 3, -3, 2, -2, 1, -1):
        sem = vrecv.at[4] if abs(k) <= 4 else vrecv.at[5]
        send(v2.at[core, slot(0)], v2.at[core, slot(-k)], vsend.at[1], sem, along(k))

    def prolong(rows):
        value = x1[rows, :] + dot(Pt[rows, :], C[...])
        x1[rows, :] = value
        db[rows, :] = value.astype(bf16)

    over_rows(prolong)

    def residual(rows):
        q[rows, :] = B[rows, :].astype(f32) - dot(K[rows, :], db[...])

    over_rows(residual)
    corr = chebyshev(lambda: None)
    trade(corr, t2, n2, tsend.at[1], trecv.at[1])
    coarse_product(v2, ys2, r2, 4, 8, 5, ysend.at[1], yrecv.at[1], 1)
    wait(n2, trecv.at[1])

    def finish(rows):
        value = D[rows, :] * zs[rows, :] + dot(Gw[rows, :], n2[...])
        y_ref[rows, :] = x1[rows, :] + value

    over_rows(finish)
    wait(r2.at[pl.ds(0, (GROUP - 1) * AGG)], yrecv.at[1])
    total = gathered_sum(r2)
    top, low = split(total)
    c_ref[0:AGG, :] = top
    c_ref[AGG : 2 * AGG, :] = low
    c_ref[2 * AGG :, :] = jnp.zeros((128 - 2 * AGG, LOADS), bf16)
    coarse_ref[...] = total

    wait(v1.at[core, pl.ds(0, 15 * AGG)], vsend.at[0])
    wait(aperm.at[0], asem)
    wait(t1, tsend.at[0])
    wait(v1.at[core], csend.at[0])
    wait(ys1.at[pl.ds(0, (GROUP - 1) * AGG)], ysend.at[0])
    wait(v2.at[core, pl.ds(0, 15 * AGG)], vsend.at[1])
    wait(v2.at[core], csend.at[1])
    wait(t2, tsend.at[1])
    wait(ys2.at[pl.ds(0, (GROUP - 1) * AGG)], ysend.at[1])


def closing(y_ref, pt_ref, c_ref, coarse_ref, out_ref, out_coarse, ys, osem):
    out_coarse[...] = coarse_ref[...]
    gives = []
    for i in range(ORDER // CHUNK):
        rows = pl.ds(i * CHUNK, CHUNK)
        ys[rows, :] = y_ref[rows, :] + dot(pt_ref[rows, :], c_ref[...])
        copy = pltpu.make_async_copy(ys.at[rows], out_ref.at[rows], osem.at[i])
        copy.start()
        gives.append(copy)
    for copy in gives:
        copy.wait()


def local(stiffness, load_cases, coarse_inverse, face_index, face_count, aggregate):
    vmem = pl.BlockSpec(memory_space=pltpu.VMEM)
    anywhere = pl.BlockSpec(memory_space=pl.ANY)
    wide_f32 = pltpu.VMEM((ORDER, LOADS), f32)
    wide_bf16 = pltpu.VMEM((ORDER, LOADS), bf16)
    square = pltpu.VMEM((CHUNK, LOADS), bf16)
    pair = pltpu.VMEM((2, CHUNK, LOADS), bf16)
    faces = pltpu.VMEM((4 * FACE, LOADS), bf16)
    hbm = pl.BlockSpec(memory_space=pltpu.HBM)
    dma = pltpu.SemaphoreType.DMA
    y, pt, c, coarse = pl.pallas_call(
        kernel,
        out_shape=(
            jax.ShapeDtypeStruct((ORDER, LOADS), f32),
            jax.ShapeDtypeStruct((ORDER, 128), bf16),
            jax.ShapeDtypeStruct((128, LOADS), bf16),
            jax.ShapeDtypeStruct((AGG, LOADS), f32),
        ),
        in_specs=[hbm, hbm, hbm, hbm, hbm, hbm],
        out_specs=(vmem, vmem, vmem, vmem),
        scratch_shapes=[
            pltpu.VMEM((ORDER, ORDER), bf16),
            wide_bf16,
            pltpu.VMEM((128, ORDER), bf16),
            wide_f32, wide_f32, wide_f32, wide_f32,
            wide_bf16, wide_bf16,
            pltpu.VMEM((4 * FACE, ORDER), bf16),
            pltpu.VMEM((ORDER, 4 * FACE), bf16),
            wide_f32,
            pltpu.VMEM((AGG, ORDER), bf16),
            pltpu.VMEM((ORDER, 128), bf16),
            pltpu.VMEM((2 * AGG, ORDER), bf16),
            pltpu.VMEM((2 * AGG, 128), bf16),
            pltpu.VMEM((1, ORDER), jnp.int32),
            pltpu.VMEM((4, FACE), jnp.int32),
            pltpu.VMEM((4, FACE), jnp.int32),
            pltpu.VMEM((2, 2, 128, CHUNK), bf16),
            pltpu.VMEM((2, 2, 128, CHUNK), bf16),
            pair, pair,
            square, square, square, square, faces, faces, faces, faces,
            pltpu.VMEM((128, LOADS), bf16),
            pltpu.VMEM((AGG, LOADS), f32),
            dma((6,)), dma, dma, dma((2,)), dma((6,)), dma((2,)), dma((2,)),
            dma((2,)), dma((2,)), dma((2,)), dma((2,)),
        ],
        compiler_params=pltpu.CompilerParams(
            collective_id=0, has_side_effects=True, vmem_limit_bytes=24 * 2**20
        ),
        name="schwarz",
    )(*[pltpu.with_memory_space_constraint(v, pltpu.HBM) for v in (stiffness[0], load_cases[0], coarse_inverse, face_index[0], face_count[0], aggregate)])
    result, coarse = pl.pallas_call(
        closing,
        out_shape=(
            jax.ShapeDtypeStruct((ORDER, LOADS), f32),
            jax.ShapeDtypeStruct((AGG, LOADS), f32),
        ),
        in_specs=[vmem, vmem, vmem, vmem],
        out_specs=(anywhere, vmem),
        scratch_shapes=[wide_f32, dma((4,))],
        compiler_params=pltpu.CompilerParams(vmem_limit_bytes=8 * 2**20),
        name="closing",
    )(y, pt, c, coarse)
    return (result[None], coarse)


def solution(mesh):
    both = ("wide", "narrow")
    placed = (
        P(both, None, None),
        P(both, None, None),
        P("wide", "narrow"),
        P(both, None, None),
        P(both, None, None),
        P(both, None),
    )
    return jax.shard_map(
        local,
        mesh=mesh,
        in_specs=placed,
        out_specs=(P(both, None, None), P(both, None)),
        check_vma=False,
    )
```

```python
import jax
import jax.numpy as jnp
from jax import lax
from jax.experimental import pallas as pl
from jax.experimental.pallas import tpu as pltpu
from jax.sharding import PartitionSpec as P

ORDER = 1024
FACE = 128
AGG = 16
LOADS = 256
CHEB = 4
DEPTH = 16
CLASSES = 4
ROWS = 8
GROUP = 2 * ROWS
HALF = LOADS // 2
BLOCK = 2 * AGG
CHUNK = 256

lower_bound = 0.8
upper_bound = 7.5
center = 0.5 * (upper_bound + lower_bound)
spread = 0.5 * (upper_bound - lower_bound)

f32 = jnp.float32
bf16 = jnp.bfloat16


def steps():
    sigma_ratio = center / spread
    rho_old = 1.0 / sigma_ratio
    factors = []
    for _ in range(CHEB - 1):
        rho_new = 1.0 / (2.0 * sigma_ratio - rho_old)
        factors.append((rho_new * rho_old, 2.0 * rho_new / spread))
        rho_old = rho_new
    return factors


FACTORS = steps()


def offsets():
    every = [(a, b, c) for a in range(4) for b in range(4) for c in range(2)]
    every = [o for o in every if o != (0, 0, 0)]
    return sorted(every, key=lambda o: -(min(o[0], 4 - o[0]) + min(o[1], 4 - o[1])))


OFFSETS = offsets()


def dot(a, b):
    return jnp.dot(a, b, preferred_element_type=f32)


def over_rows(body, size=CHUNK, total=ORDER):
    for i in range(total // size):
        body(slice(i * size, (i + 1) * size))


def split(value):
    high = value.astype(bf16)
    return high, (value - high.astype(f32)).astype(bf16)


def transposed_row(row):
    return jnp.transpose(jnp.broadcast_to(row.astype(f32), (128, 128)))


def fill_prolongation(agg_ref, into):
    lane = lax.broadcasted_iota(jnp.int32, (128, 128), 1)
    member = jnp.where(lane < 2 * AGG, lane % AGG, -1).astype(f32)
    for i in range(ORDER // 128):
        column = transposed_row(agg_ref[:, i * 128 : (i + 1) * 128])
        into[i * 128 : (i + 1) * 128, :] = jnp.where(column == member, 1.0, 0.0).astype(bf16)


def kernel(
    stiffness, loads, inverse, indices, counts, groups,
    y_ref, pt_ref, c_ref, coarse_ref,
    K, B, A, q, d, zs, x1, da, db, G, Gw, D, Pm, Pt, PK, S,
    aggregate, face_index, face_count, aperm, A2, u1, u2, v1, v2, ys1, ys2, r1, r2, t1, t2, n1, n2, C, pb,
    lsem, asem, arecv, vsend, vrecv, ysend, yrecv, tsend, trecv,
):
    load_b = pltpu.make_async_copy(loads, B, lsem.at[0])
    load_k = pltpu.make_async_copy(stiffness, K, lsem.at[2])
    load_a = pltpu.make_async_copy(inverse, A, lsem.at[1])
    load_g = pltpu.make_async_copy(groups, aggregate, lsem.at[3])
    load_i = pltpu.make_async_copy(indices, face_index, lsem.at[4])
    load_c = pltpu.make_async_copy(counts, face_count, lsem.at[5])
    load_g.start()
    load_b.start()

    w = lax.axis_index("wide")
    n = lax.axis_index("narrow")
    z = w // 4
    y = ((w // 2) % 2) * 2 + n % 2
    x = n // 2
    high = (w // 2) % 2
    core = w % 2

    def along(k, c=None):
        c = core if c is None else c
        return (((z + DEPTH + k) % DEPTH) * 4 + high * 2 + c, n)

    def slot(k):
        return pl.ds((k % DEPTH) * BLOCK, BLOCK)

    def part(k, c):
        return pl.ds(pl.multiple_of((k % DEPTH) * BLOCK + c * AGG, AGG), AGG)

    def member(o):
        yy = (y + o[1]) % 4
        cc = (core + o[2]) % 2
        nn = ((x + o[0]) % 4) * 2 + yy % 2
        up = yy // 2
        return (z * 4 + up * 2 + cc, nn), (up * 2 + cc) * ROWS + nn

    def group_rows(index):
        return pl.ds(pl.multiple_of(index * AGG, AGG), AGG)

    cls = high * 2 + core
    own = core * GROUP + high * ROWS + n
    sides = [((w + 63) % 64, n), ((w + 1) % 64, n), (w, (n + 7) % 8), (w, (n + 1) % 8)]

    barrier = pltpu.get_barrier_semaphore()
    greeted = [along(s * k, c) for k in (4, 3, 2, 1) for s in (1, -1) for c in (0, 1)]
    greeted = greeted + [member(o)[0] for o in OFFSETS] + sides[:2]
    for peer in greeted:
        pl.semaphore_signal(barrier, inc=1, device_id=peer, device_id_type=pl.DeviceIdType.MESH)
    load_k.start()
    load_a.start()
    load_i.start()
    load_c.start()

    def send(src, dst, ssem, rsem, peer):
        pltpu.make_async_remote_copy(
            src_ref=src, dst_ref=dst, send_sem=ssem, recv_sem=rsem,
            device_id=peer, device_id_type=pl.DeviceIdType.MESH,
        ).start()

    def wait(ref, sem):
        pltpu.make_async_copy(ref, ref, sem).wait()

    load_g.wait()
    sub16 = lax.broadcasted_iota(jnp.int32, (AGG, ORDER), 0)
    Pm[...] = jnp.where(sub16 == aggregate[...], 1.0, 0.0).astype(bf16)
    load_b.wait()
    first = dot(Pm[...], B[...])
    pb[...] = first

    def offer(u, v, value, i):
        for c in range(2):
            u[c] = value[:, c * HALF : (c + 1) * HALF].astype(bf16)
        v[part(0, core), :] = u[core]

    def spread(u, v, distances, sem_of, i):
        for k in distances:
            for c in range(2):
                send(u.at[c], v.at[part(-k, core)], vsend.at[i], sem_of(k), along(k, c))
        send(u.at[1 - core], v.at[part(0, core)], vsend.at[i], sem_of(0), along(0, 1 - core))

    offer(u1, v1, first, 0)
    pl.semaphore_wait(barrier, len(greeted))

    def first_sem(k):
        return vrecv.at[0] if k == 4 else vrecv.at[1] if k == -4 else vrecv.at[2]

    spread(u1, v1, (4, -4, 3, -3, 2, -2, 1, -1), first_sem, 0)

    load_a.wait()
    for j in range(2):
        for part_of in range(2):
            place = lax.broadcasted_iota(jnp.int32, (CHUNK, CHUNK), 1) + part_of * CHUNK
            place = ((place // BLOCK + z) % DEPTH) * (2 * BLOCK) + j * BLOCK + place % BLOCK
            row = lax.broadcasted_iota(jnp.int32, (CHUNK, CHUNK), 0)
            total = jnp.zeros((128, CHUNK), f32)
            for t in range(4):
                pick = jnp.where(row + t * CHUNK == place, 1.0, 0.0).astype(bf16)
                total = total + dot(A[:, t * CHUNK : (t + 1) * CHUNK], pick)
            aperm[j, :, part_of * CHUNK : (part_of + 1) * CHUNK] = total.astype(bf16)
    for up, c in ((1, 1), (1, 0), (0, 1)):
        hh = (high + up) % 2
        target = (z * 4 + hh * 2 + (core + c) % 2, n)
        send(aperm.at[hh], A2.at[cls], asem, arecv, target)
    A2[cls] = aperm[high]

    def chebyshev(after_second):
        def begin(rows):
            da[rows, :] = (q[rows, :] * (1.0 / center)).astype(bf16)

        over_rows(begin)
        for s, (keep, gain) in enumerate(FACTORS):
            src, dst = (da, db) if s % 2 == 0 else (db, da)

            def step(rows, s=s, keep=keep, gain=gain, src=src, dst=dst):
                before = q[rows, :]
                left = before - dot(K[rows, :], src[...])
                old = before * (1.0 / center) if s == 0 else d[rows, :]
                result = old if s == 0 else zs[rows, :]
                new = keep * old + gain * left
                if s < CHEB - 2:
                    q[rows, :] = left
                    d[rows, :] = new
                zs[rows, :] = result + new
                dst[rows, :] = (new if s < CHEB - 2 else result + new).astype(bf16)

            over_rows(step)
            if s == 1:
                after_second()
        return db

    def trade(corr, t, nb, tsem, rsem):
        t[...] = dot(G[...], corr[...]).astype(bf16)
        for f, target in ((0, 1), (1, 0), (2, 3), (3, 2)):
            send(
                t.at[pl.ds(f * FACE, FACE)], nb.at[pl.ds(target * FACE, FACE)], tsem, rsem,
                sides[f],
            )

    def relay():
        wait(v1.at[slot(-4)], vrecv.at[0])
        for k in (4, 3, 2, 1):
            send(v1.at[slot(-4)], v1.at[slot(-4 - k)], vsend.at[0], vrecv.at[2], along(k))
        wait(v1.at[slot(4)], vrecv.at[1])
        for k in (3, 2, 1):
            send(v1.at[slot(4)], v1.at[slot(4 + k)], vsend.at[0], vrecv.at[2], along(-k))

    def coarse_product(v, ys, r, blocks, vsem, ssem, rsem, i):
        wait(v.at[pl.ds(0, blocks * AGG)], vsem)
        if i == 0:
            wait(A2.at[pl.ds(0, 3)], arecv)
        for j in range(2):
            value = dot(A2[2 * j : 2 * j + 2].reshape(CHUNK, 2 * CHUNK), v[...])
            ys[j * CHUNK : (j + 1) * CHUNK, :] = value.astype(bf16)
        for o in OFFSETS:
            peer, index = member(o)
            send(ys.at[group_rows(index)], r.at[group_rows(own)], ssem, rsem, peer)
        r[group_rows(own), :] = ys[group_rows(cls * ROWS + n), :]

    def gathered_sum(r):
        halves = []
        for c in range(2):
            total = r[c * CHUNK : c * CHUNK + AGG, :].astype(f32)
            for i in range(1, GROUP):
                total = total + r[c * CHUNK + i * AGG : c * CHUNK + (i + 1) * AGG, :].astype(f32)
            halves.append(total)
        return jnp.concatenate(halves, axis=1)

    def to_f32(rows):
        q[rows, :] = B[rows, :].astype(f32)

    over_rows(to_f32)
    load_k.wait()
    corr = chebyshev(relay)

    load_i.wait()
    load_c.wait()
    lane = lax.broadcasted_iota(jnp.int32, (128, 128), 1).astype(f32)
    sub = lax.broadcasted_iota(jnp.int32, (128, 128), 0).astype(f32)
    there = [w > 0, w < 63, n > 0, n < 7]
    for f in range(4):
        row = face_index[f : f + 1, :].astype(f32)
        column = transposed_row(row)
        weight = (4 - face_count[f : f + 1, :]).astype(f32) * 0.25
        weight = weight * jnp.where(there[f], 1.0, 0.0)
        for i in range(8):
            hit = jnp.where(column == lane + 128.0 * i, 1.0, 0.0)
            G[f * 128 : (f + 1) * 128, i * 128 : (i + 1) * 128] = hit.astype(bf16)
            hit = jnp.where(row == sub + 128.0 * i, weight, 0.0)
            Gw[i * 128 : (i + 1) * 128, f * 128 : (f + 1) * 128] = hit.astype(bf16)
    trade(corr, t1, n1, tsend.at[0], trecv.at[0])

    fill_prolongation(aggregate, Pt)
    top, low = split(dot(Pm[...], K[...]))
    PK[0:AGG, :] = top
    PK[AGG : 2 * AGG, :] = low
    both = dot(PK[...], Pt[...])
    top, low = split(both[0:AGG] + both[AGG : 2 * AGG])
    S[0:AGG, :] = top
    S[AGG : 2 * AGG, :] = low
    C[2 * AGG :, :] = jnp.zeros((128 - 2 * AGG, LOADS), bf16)
    pt_ref[...] = Pt[...]

    coarse_product(v1, ys1, r1, 27, vrecv.at[2], ysend.at[0], yrecv.at[0], 0)

    def keep_share(rows):
        D[rows, :] = 1.0 - dot(Gw[rows, :], jnp.ones((4 * FACE, LOADS), bf16))

    over_rows(keep_share)
    wait(n1, trecv.at[0])

    def average(rows):
        value = D[rows, :] * zs[rows, :] + dot(Gw[rows, :], n1[...])
        x1[rows, :] = value
        da[rows, :] = value.astype(bf16)

    over_rows(average)
    both = dot(PK[...], da[...])
    pb[...] = pb[...] - both[0:AGG] - both[AGG : 2 * AGG]

    wait(r1.at[pl.ds(0, (2 * GROUP - 1) * AGG)], yrecv.at[0])
    top, low = split(gathered_sum(r1))
    C[0:AGG, :] = top
    C[AGG : 2 * AGG, :] = low
    both = dot(S[...], C[...])
    offer(u2, v2, pb[...] - both[0:AGG] - both[AGG : 2 * AGG], 1)
    send(u2.at[1 - core], v2.at[part(0, core)], vsend.at[1], vrecv.at[3], along(0, 1 - core))
    for i in range(DEPTH - 1):
        target = i + (i + DEPTH - z) // DEPTH
        place = (z - target + DEPTH) % DEPTH
        for c in range(2):
            send(
                u2.at[c], v2.at[part(place, core)], vsend.at[1], vrecv.at[3],
                (target * 4 + high * 2 + c, n),
            )

    def prolong(rows):
        value = x1[rows, :] + dot(Pt[rows, :], C[...])
        x1[rows, :] = value
        db[rows, :] = value.astype(bf16)

    over_rows(prolong)

    def residual(rows):
        q[rows, :] = B[rows, :].astype(f32) - dot(K[rows, :], db[...])

    over_rows(residual)
    corr = chebyshev(lambda: None)
    trade(corr, t2, n2, tsend.at[1], trecv.at[1])
    coarse_product(v2, ys2, r2, 31, vrecv.at[3], ysend.at[1], yrecv.at[1], 1)
    wait(n2, trecv.at[1])

    def finish(rows):
        value = D[rows, :] * zs[rows, :] + dot(Gw[rows, :], n2[...])
        y_ref[rows, :] = x1[rows, :] + value

    over_rows(finish)
    wait(r2.at[pl.ds(0, (2 * GROUP - 1) * AGG)], yrecv.at[1])
    total = gathered_sum(r2)
    top, low = split(total)
    c_ref[0:AGG, :] = top
    c_ref[AGG : 2 * AGG, :] = low
    c_ref[2 * AGG :, :] = jnp.zeros((128 - 2 * AGG, LOADS), bf16)
    coarse_ref[...] = total

    wait(v1.at[pl.ds(0, 31 * AGG)], vsend.at[0])
    wait(A2.at[pl.ds(0, 3)], asem)
    wait(t1, tsend.at[0])
    wait(ys1.at[pl.ds(0, (2 * GROUP - 1) * AGG)], ysend.at[0])
    wait(v2.at[pl.ds(0, 31 * AGG)], vsend.at[1])
    wait(t2, tsend.at[1])
    wait(ys2.at[pl.ds(0, (2 * GROUP - 1) * AGG)], ysend.at[1])


def closing(y_ref, pt_ref, c_ref, coarse_ref, out_ref, out_coarse, ys, osem):
    out_coarse[...] = coarse_ref[...]
    gives = []
    for i in range(ORDER // CHUNK):
        rows = pl.ds(i * CHUNK, CHUNK)
        ys[rows, :] = y_ref[rows, :] + dot(pt_ref[rows, :], c_ref[...])
        copy = pltpu.make_async_copy(ys.at[rows], out_ref.at[rows], osem.at[i])
        copy.start()
        gives.append(copy)
    for copy in gives:
        copy.wait()


def local(stiffness, load_cases, coarse_inverse, face_index, face_count, aggregate):
    vmem = pl.BlockSpec(memory_space=pltpu.VMEM)
    anywhere = pl.BlockSpec(memory_space=pl.ANY)
    wide_f32 = pltpu.VMEM((ORDER, LOADS), f32)
    wide_bf16 = pltpu.VMEM((ORDER, LOADS), bf16)
    pair = pltpu.VMEM((2, AGG, HALF), bf16)
    tall = pltpu.VMEM((2 * CHUNK, HALF), bf16)
    faces = pltpu.VMEM((4 * FACE, LOADS), bf16)
    hbm = pl.BlockSpec(memory_space=pltpu.HBM)
    dma = pltpu.SemaphoreType.DMA
    y, pt, c, coarse = pl.pallas_call(
        kernel,
        out_shape=(
            jax.ShapeDtypeStruct((ORDER, LOADS), f32),
            jax.ShapeDtypeStruct((ORDER, 128), bf16),
            jax.ShapeDtypeStruct((128, LOADS), bf16),
            jax.ShapeDtypeStruct((AGG, LOADS), f32),
        ),
        in_specs=[hbm, hbm, hbm, hbm, hbm, hbm],
        out_specs=(vmem, vmem, vmem, vmem),
        scratch_shapes=[
            pltpu.VMEM((ORDER, ORDER), bf16),
            wide_bf16,
            pltpu.VMEM((128, ORDER), bf16),
            wide_f32, wide_f32, wide_f32, wide_f32,
            wide_bf16, wide_bf16,
            pltpu.VMEM((4 * FACE, ORDER), bf16),
            pltpu.VMEM((ORDER, 4 * FACE), bf16),
            wide_f32,
            pltpu.VMEM((AGG, ORDER), bf16),
            pltpu.VMEM((ORDER, 128), bf16),
            pltpu.VMEM((2 * AGG, ORDER), bf16),
            pltpu.VMEM((2 * AGG, 128), bf16),
            pltpu.VMEM((1, ORDER), jnp.int32),
            pltpu.VMEM((4, FACE), jnp.int32),
            pltpu.VMEM((4, FACE), jnp.int32),
            pltpu.VMEM((2, 128, 2 * CHUNK), bf16),
            pltpu.VMEM((CLASSES, 128, 2 * CHUNK), bf16),
            pair, pair, tall, tall,
            tall, tall, tall, tall, faces, faces, faces, faces,
            pltpu.VMEM((128, LOADS), bf16),
            pltpu.VMEM((AGG, LOADS), f32),
            dma((6,)), dma, dma, dma((2,)), dma((4,)),
            dma((2,)), dma((2,)), dma((2,)), dma((2,)),
        ],
        compiler_params=pltpu.CompilerParams(
            collective_id=0, has_side_effects=True, vmem_limit_bytes=24 * 2**20
        ),
        name="schwarz",
    )(*[pltpu.with_memory_space_constraint(v, pltpu.HBM) for v in (stiffness[0], load_cases[0], coarse_inverse, face_index[0], face_count[0], aggregate)])
    result, coarse = pl.pallas_call(
        closing,
        out_shape=(
            jax.ShapeDtypeStruct((ORDER, LOADS), f32),
            jax.ShapeDtypeStruct((AGG, LOADS), f32),
        ),
        in_specs=[vmem, vmem, vmem, vmem],
        out_specs=(anywhere, vmem),
        scratch_shapes=[wide_f32, dma((4,))],
        compiler_params=pltpu.CompilerParams(vmem_limit_bytes=8 * 2**20),
        name="closing",
    )(y, pt, c, coarse)
    return (result[None], coarse)


def solution(mesh):
    both = ("wide", "narrow")
    placed = (
        P(both, None, None),
        P(both, None, None),
        P("wide", "narrow"),
        P(both, None, None),
        P(both, None, None),
        P(both, None),
    )
    return jax.shard_map(
        local,
        mesh=mesh,
        in_specs=placed,
        out_specs=(P(both, None, None), P(both, None)),
        check_vma=False,
    )
```

```python
import jax
import jax.numpy as jnp
from jax import lax
from jax.experimental import pallas as pl
from jax.experimental.pallas import tpu as pltpu
from jax.sharding import PartitionSpec as P

ORDER = 1024
FACE = 128
AGG = 16
LOADS = 256
CHEB = 4
DEPTH = 16
CLASSES = 4
ROWS = 8
GROUP = 2 * ROWS
HALF = LOADS // 2
BLOCK = 2 * AGG
CHUNK = 256

lower_bound = 0.8
upper_bound = 7.5
center = 0.5 * (upper_bound + lower_bound)
spread = 0.5 * (upper_bound - lower_bound)

f32 = jnp.float32
bf16 = jnp.bfloat16


def steps():
    sigma_ratio = center / spread
    rho_old = 1.0 / sigma_ratio
    factors = []
    for _ in range(CHEB - 1):
        rho_new = 1.0 / (2.0 * sigma_ratio - rho_old)
        factors.append((rho_new * rho_old, 2.0 * rho_new / spread))
        rho_old = rho_new
    return factors


FACTORS = steps()


def offsets():
    every = [(a, b, c) for a in range(4) for b in range(4) for c in range(2)]
    every = [o for o in every if o != (0, 0, 0)]
    return sorted(every, key=lambda o: -(min(o[0], 4 - o[0]) + min(o[1], 4 - o[1])))


OFFSETS = offsets()


def dot(a, b):
    return jnp.dot(a, b, preferred_element_type=f32)


def over_rows(body, size=CHUNK, total=ORDER):
    for i in range(total // size):
        body(slice(i * size, (i + 1) * size))


def split(value):
    high = value.astype(bf16)
    return high, (value - high.astype(f32)).astype(bf16)


def transposed_row(row):
    return jnp.transpose(jnp.broadcast_to(row.astype(f32), (128, 128)))


def fill_prolongation(agg_ref, into):
    lane = lax.broadcasted_iota(jnp.int32, (128, 128), 1)
    member = jnp.where(lane < 2 * AGG, lane % AGG, -1).astype(f32)
    for i in range(ORDER // 128):
        column = transposed_row(agg_ref[:, i * 128 : (i + 1) * 128])
        into[i * 128 : (i + 1) * 128, :] = jnp.where(column == member, 1.0, 0.0).astype(bf16)


def kernel(
    stiffness, loads, inverse, indices, counts, groups,
    y_ref, pt_ref, c_ref, coarse_ref,
    K, B, A, q, d, zs, x1, da, db, G, Gw, D, Pm, Pt, PK, S,
    aggregate, face_index, face_count, aperm, A2, u1, u2, v1, v2, ys1, ys2, r1, r2, t1, t2, n1, n2, C, pb,
    lsem, asem, arecv, vsend, vrecv, ysend, yrecv, tsend, trecv,
):
    load_b = pltpu.make_async_copy(loads, B, lsem.at[0])
    load_k = pltpu.make_async_copy(stiffness, K, lsem.at[2])
    load_a = pltpu.make_async_copy(inverse, A, lsem.at[1])
    load_g = pltpu.make_async_copy(groups, aggregate, lsem.at[3])
    load_i = pltpu.make_async_copy(indices, face_index, lsem.at[4])
    load_c = pltpu.make_async_copy(counts, face_count, lsem.at[5])
    load_g.start()
    load_b.start()

    w = lax.axis_index("wide")
    n = lax.axis_index("narrow")
    z = w // 4
    y = ((w // 2) % 2) * 2 + n % 2
    x = n // 2
    high = (w // 2) % 2
    core = w % 2

    def along(k, c=None):
        c = core if c is None else c
        return (((z + DEPTH + k) % DEPTH) * 4 + high * 2 + c, n)

    def slot(k):
        return pl.ds((k % DEPTH) * BLOCK, BLOCK)

    def part(k, c):
        return pl.ds(pl.multiple_of((k % DEPTH) * BLOCK + c * AGG, AGG), AGG)

    def member(o):
        yy = (y + o[1]) % 4
        cc = (core + o[2]) % 2
        nn = ((x + o[0]) % 4) * 2 + yy % 2
        up = yy // 2
        return (z * 4 + up * 2 + cc, nn), (up * 2 + cc) * ROWS + nn

    def group_rows(index):
        return pl.ds(pl.multiple_of(index * AGG, AGG), AGG)

    cls = high * 2 + core
    own = core * GROUP + high * ROWS + n
    sides = [((w + 63) % 64, n), ((w + 1) % 64, n), (w, (n + 7) % 8), (w, (n + 1) % 8)]

    barrier = pltpu.get_barrier_semaphore()
    greeted = [along(s * k, c) for k in (4, 3, 2, 1) for s in (1, -1) for c in (0, 1)]
    greeted = greeted + [member(o)[0] for o in OFFSETS] + sides[:2]
    for peer in greeted:
        pl.semaphore_signal(barrier, inc=1, device_id=peer, device_id_type=pl.DeviceIdType.MESH)
    load_k.start()
    load_a.start()
    load_i.start()
    load_c.start()

    def send(src, dst, ssem, rsem, peer):
        pltpu.make_async_remote_copy(
            src_ref=src, dst_ref=dst, send_sem=ssem, recv_sem=rsem,
            device_id=peer, device_id_type=pl.DeviceIdType.MESH,
        ).start()

    def wait(ref, sem):
        pltpu.make_async_copy(ref, ref, sem).wait()

    load_g.wait()
    sub16 = lax.broadcasted_iota(jnp.int32, (AGG, ORDER), 0)
    Pm[...] = jnp.where(sub16 == aggregate[...], 1.0, 0.0).astype(bf16)
    load_b.wait()
    first = dot(Pm[...], B[...])
    pb[...] = first

    def offer(u, v, value, i):
        for c in range(2):
            u[c] = value[:, c * HALF : (c + 1) * HALF].astype(bf16)
        v[part(0, core), :] = u[core]

    def spread(u, v, distances, sem_of, i):
        for k in distances:
            for c in range(2):
                send(u.at[c], v.at[part(-k, core)], vsend.at[i], sem_of(k), along(k, c))
        send(u.at[1 - core], v.at[part(0, core)], vsend.at[i], sem_of(0), along(0, 1 - core))

    offer(u1, v1, first, 0)
    pl.semaphore_wait(barrier, len(greeted))

    def first_sem(k):
        return vrecv.at[0] if k == 4 else vrecv.at[1] if k == -4 else vrecv.at[2]

    spread(u1, v1, (4, -4, 3, -3, 2, -2, 1, -1), first_sem, 0)

    load_a.wait()
    for j in range(2):
        for part_of in range(2):
            place = lax.broadcasted_iota(jnp.int32, (CHUNK, CHUNK), 1) + part_of * CHUNK
            place = ((place // BLOCK + z) % DEPTH) * (2 * BLOCK) + j * BLOCK + place % BLOCK
            row = lax.broadcasted_iota(jnp.int32, (CHUNK, CHUNK), 0)
            total = jnp.zeros((128, CHUNK), f32)
            for t in range(4):
                pick = jnp.where(row + t * CHUNK == place, 1.0, 0.0).astype(bf16)
                total = total + dot(A[:, t * CHUNK : (t + 1) * CHUNK], pick)
            aperm[j, :, part_of * CHUNK : (part_of + 1) * CHUNK] = total.astype(bf16)
    for up, c in ((1, 1), (1, 0), (0, 1)):
        hh = (high + up) % 2
        target = (z * 4 + hh * 2 + (core + c) % 2, n)
        send(aperm.at[hh], A2.at[cls], asem, arecv, target)
    A2[cls] = aperm[high]

    def chebyshev(after_second):
        def begin(rows):
            da[rows, :] = (q[rows, :] * (1.0 / center)).astype(bf16)

        over_rows(begin)
        for s, (keep, gain) in enumerate(FACTORS):
            src, dst = (da, db) if s % 2 == 0 else (db, da)

            def step(rows, s=s, keep=keep, gain=gain, src=src, dst=dst):
                before = q[rows, :]
                left = before - dot(K[rows, :], src[...])
                old = before * (1.0 / center) if s == 0 else d[rows, :]
                result = old if s == 0 else zs[rows, :]
                new = keep * old + gain * left
                if s < CHEB - 2:
                    q[rows, :] = left
                    d[rows, :] = new
                zs[rows, :] = result + new
                dst[rows, :] = (new if s < CHEB - 2 else result + new).astype(bf16)

            over_rows(step)
            if s == 0:
                after_second()
        return db

    def trade(corr, t, nb, tsem, rsem):
        t[...] = dot(G[...], corr[...]).astype(bf16)
        for f, target in ((0, 1), (1, 0), (2, 3), (3, 2)):
            send(
                t.at[pl.ds(f * FACE, FACE)], nb.at[pl.ds(target * FACE, FACE)], tsem, rsem,
                sides[f],
            )

    def relay():
        wait(v1.at[slot(-4)], vrecv.at[0])
        for k in (4, 3, 2, 1):
            send(v1.at[slot(-4)], v1.at[slot(-4 - k)], vsend.at[0], vrecv.at[2], along(k))
        wait(v1.at[slot(4)], vrecv.at[1])
        for k in (3, 2, 1):
            send(v1.at[slot(4)], v1.at[slot(4 + k)], vsend.at[0], vrecv.at[2], along(-k))

    def coarse_product(v, ys, r, blocks, vsem, ssem, rsem, i):
        wait(v.at[pl.ds(0, blocks * AGG)], vsem)
        if i == 0:
            wait(A2.at[pl.ds(0, 3)], arecv)
        for j in range(2):
            value = dot(A2[2 * j : 2 * j + 2].reshape(CHUNK, 2 * CHUNK), v[...])
            ys[j * CHUNK : (j + 1) * CHUNK, :] = value.astype(bf16)
        for o in OFFSETS:
            peer, index = member(o)
            send(ys.at[group_rows(index)], r.at[group_rows(own)], ssem, rsem, peer)
        r[group_rows(own), :] = ys[group_rows(cls * ROWS + n), :]

    def gathered_sum(r):
        halves = []
        for c in range(2):
            total = r[c * CHUNK : c * CHUNK + AGG, :].astype(f32)
            for i in range(1, GROUP):
                total = total + r[c * CHUNK + i * AGG : c * CHUNK + (i + 1) * AGG, :].astype(f32)
            halves.append(total)
        return jnp.concatenate(halves, axis=1)

    def to_f32(rows):
        q[rows, :] = B[rows, :].astype(f32)

    over_rows(to_f32)
    load_k.wait()
    corr = chebyshev(relay)

    load_i.wait()
    load_c.wait()
    lane = lax.broadcasted_iota(jnp.int32, (128, 128), 1).astype(f32)
    sub = lax.broadcasted_iota(jnp.int32, (128, 128), 0).astype(f32)
    there = [w > 0, w < 63, n > 0, n < 7]
    for f in range(4):
        row = face_index[f : f + 1, :].astype(f32)
        column = transposed_row(row)
        weight = (4 - face_count[f : f + 1, :]).astype(f32) * 0.25
        weight = weight * jnp.where(there[f], 1.0, 0.0)
        for i in range(8):
            hit = jnp.where(column == lane + 128.0 * i, 1.0, 0.0)
            G[f * 128 : (f + 1) * 128, i * 128 : (i + 1) * 128] = hit.astype(bf16)
            hit = jnp.where(row == sub + 128.0 * i, weight, 0.0)
            Gw[i * 128 : (i + 1) * 128, f * 128 : (f + 1) * 128] = hit.astype(bf16)
    trade(corr, t1, n1, tsend.at[0], trecv.at[0])

    fill_prolongation(aggregate, Pt)
    top, low = split(dot(Pm[...], K[...]))
    PK[0:AGG, :] = top
    PK[AGG : 2 * AGG, :] = low
    both = dot(PK[...], Pt[...])
    top, low = split(both[0:AGG] + both[AGG : 2 * AGG])
    S[0:AGG, :] = top
    S[AGG : 2 * AGG, :] = low
    C[2 * AGG :, :] = jnp.zeros((128 - 2 * AGG, LOADS), bf16)
    pt_ref[...] = Pt[...]

    coarse_product(v1, ys1, r1, 27, vrecv.at[2], ysend.at[0], yrecv.at[0], 0)

    def keep_share(rows):
        D[rows, :] = 1.0 - dot(Gw[rows, :], jnp.ones((4 * FACE, LOADS), bf16))

    over_rows(keep_share)
    wait(n1, trecv.at[0])

    def average(rows):
        value = D[rows, :] * zs[rows, :] + dot(Gw[rows, :], n1[...])
        x1[rows, :] = value
        da[rows, :] = value.astype(bf16)

    over_rows(average)
    both = dot(PK[...], da[...])
    pb[...] = pb[...] - both[0:AGG] - both[AGG : 2 * AGG]

    wait(r1.at[pl.ds(0, (2 * GROUP - 1) * AGG)], yrecv.at[0])
    top, low = split(gathered_sum(r1))
    C[0:AGG, :] = top
    C[AGG : 2 * AGG, :] = low
    both = dot(S[...], C[...])
    offer(u2, v2, pb[...] - both[0:AGG] - both[AGG : 2 * AGG], 1)
    send(u2.at[1 - core], v2.at[part(0, core)], vsend.at[1], vrecv.at[3], along(0, 1 - core))
    for i in range(DEPTH - 1):
        target = i + (i + DEPTH - z) // DEPTH
        place = (z - target + DEPTH) % DEPTH
        for c in range(2):
            send(
                u2.at[c], v2.at[part(place, core)], vsend.at[1], vrecv.at[3],
                (target * 4 + high * 2 + c, n),
            )

    def prolong(rows):
        value = x1[rows, :] + dot(Pt[rows, :], C[...])
        x1[rows, :] = value
        db[rows, :] = value.astype(bf16)

    over_rows(prolong)

    def residual(rows):
        q[rows, :] = B[rows, :].astype(f32) - dot(K[rows, :], db[...])

    over_rows(residual)
    corr = chebyshev(lambda: None)
    trade(corr, t2, n2, tsend.at[1], trecv.at[1])
    coarse_product(v2, ys2, r2, 31, vrecv.at[3], ysend.at[1], yrecv.at[1], 1)
    wait(n2, trecv.at[1])

    def finish(rows):
        value = D[rows, :] * zs[rows, :] + dot(Gw[rows, :], n2[...])
        y_ref[rows, :] = x1[rows, :] + value

    over_rows(finish)
    wait(r2.at[pl.ds(0, (2 * GROUP - 1) * AGG)], yrecv.at[1])
    total = gathered_sum(r2)
    top, low = split(total)
    c_ref[0:AGG, :] = top
    c_ref[AGG : 2 * AGG, :] = low
    c_ref[2 * AGG :, :] = jnp.zeros((128 - 2 * AGG, LOADS), bf16)
    coarse_ref[...] = total

    wait(v1.at[pl.ds(0, 31 * AGG)], vsend.at[0])
    wait(A2.at[pl.ds(0, 3)], asem)
    wait(t1, tsend.at[0])
    wait(ys1.at[pl.ds(0, (2 * GROUP - 1) * AGG)], ysend.at[0])
    wait(v2.at[pl.ds(0, 31 * AGG)], vsend.at[1])
    wait(t2, tsend.at[1])
    wait(ys2.at[pl.ds(0, (2 * GROUP - 1) * AGG)], ysend.at[1])


def closing(y_ref, pt_ref, c_ref, coarse_ref, out_ref, out_coarse, ys, osem):
    out_coarse[...] = coarse_ref[...]
    gives = []
    for i in range(ORDER // CHUNK):
        rows = pl.ds(i * CHUNK, CHUNK)
        ys[rows, :] = y_ref[rows, :] + dot(pt_ref[rows, :], c_ref[...])
        copy = pltpu.make_async_copy(ys.at[rows], out_ref.at[rows], osem.at[i])
        copy.start()
        gives.append(copy)
    for copy in gives:
        copy.wait()


def local(stiffness, load_cases, coarse_inverse, face_index, face_count, aggregate):
    vmem = pl.BlockSpec(memory_space=pltpu.VMEM)
    anywhere = pl.BlockSpec(memory_space=pl.ANY)
    wide_f32 = pltpu.VMEM((ORDER, LOADS), f32)
    wide_bf16 = pltpu.VMEM((ORDER, LOADS), bf16)
    pair = pltpu.VMEM((2, AGG, HALF), bf16)
    tall = pltpu.VMEM((2 * CHUNK, HALF), bf16)
    faces = pltpu.VMEM((4 * FACE, LOADS), bf16)
    hbm = pl.BlockSpec(memory_space=pltpu.HBM)
    dma = pltpu.SemaphoreType.DMA
    y, pt, c, coarse = pl.pallas_call(
        kernel,
        out_shape=(
            jax.ShapeDtypeStruct((ORDER, LOADS), f32),
            jax.ShapeDtypeStruct((ORDER, 128), bf16),
            jax.ShapeDtypeStruct((128, LOADS), bf16),
            jax.ShapeDtypeStruct((AGG, LOADS), f32),
        ),
        in_specs=[hbm, hbm, hbm, hbm, hbm, hbm],
        out_specs=(vmem, vmem, vmem, vmem),
        scratch_shapes=[
            pltpu.VMEM((ORDER, ORDER), bf16),
            wide_bf16,
            pltpu.VMEM((128, ORDER), bf16),
            wide_f32, wide_f32, wide_f32, wide_f32,
            wide_bf16, wide_bf16,
            pltpu.VMEM((4 * FACE, ORDER), bf16),
            pltpu.VMEM((ORDER, 4 * FACE), bf16),
            wide_f32,
            pltpu.VMEM((AGG, ORDER), bf16),
            pltpu.VMEM((ORDER, 128), bf16),
            pltpu.VMEM((2 * AGG, ORDER), bf16),
            pltpu.VMEM((2 * AGG, 128), bf16),
            pltpu.VMEM((1, ORDER), jnp.int32),
            pltpu.VMEM((4, FACE), jnp.int32),
            pltpu.VMEM((4, FACE), jnp.int32),
            pltpu.VMEM((2, 128, 2 * CHUNK), bf16),
            pltpu.VMEM((CLASSES, 128, 2 * CHUNK), bf16),
            pair, pair, tall, tall,
            tall, tall, tall, tall, faces, faces, faces, faces,
            pltpu.VMEM((128, LOADS), bf16),
            pltpu.VMEM((AGG, LOADS), f32),
            dma((6,)), dma, dma, dma((2,)), dma((4,)),
            dma((2,)), dma((2,)), dma((2,)), dma((2,)),
        ],
        compiler_params=pltpu.CompilerParams(
            collective_id=0, has_side_effects=True, vmem_limit_bytes=24 * 2**20
        ),
        name="schwarz",
    )(*[pltpu.with_memory_space_constraint(v, pltpu.HBM) for v in (stiffness[0], load_cases[0], coarse_inverse, face_index[0], face_count[0], aggregate)])
    result, coarse = pl.pallas_call(
        closing,
        out_shape=(
            jax.ShapeDtypeStruct((ORDER, LOADS), f32),
            jax.ShapeDtypeStruct((AGG, LOADS), f32),
        ),
        in_specs=[vmem, vmem, vmem, vmem],
        out_specs=(anywhere, vmem),
        scratch_shapes=[wide_f32, dma((4,))],
        compiler_params=pltpu.CompilerParams(vmem_limit_bytes=8 * 2**20),
        name="closing",
    )(y, pt, c, coarse)
    return (result[None], coarse)


def solution(mesh):
    both = ("wide", "narrow")
    placed = (
        P(both, None, None),
        P(both, None, None),
        P("wide", "narrow"),
        P(both, None, None),
        P(both, None, None),
        P(both, None),
    )
    return jax.shard_map(
        local,
        mesh=mesh,
        in_specs=placed,
        out_specs=(P(both, None, None), P(both, None)),
        check_vma=False,
    )
```
